32 devices in a mesh: row: 4 (over y, core), blk: 8 (over z, x).
Axes of the slice: x: 2, y: 2, z: 4, core: 2. Of those that a mesh axis runs over, the one named last changes fastest.
Arguments:
- matrix: float32 [16384, 2048], P('row', 'blk'), may hold values from -6 to 6
Outputs:
- rotated: float32 [16384, 2048], P('row', 'blk')
- off_measure: float32 [2], replicated
The draws below stay inside these ranges and needn't reach their ends.
All inputs are finite; a program needn't handle non-finite values.
Results may differ from the reference program's by a relative error of at most 0.00012.
Values sent between devices are 32-bit elements; how exact they have to be, the bound alone decides.
A program may use at most 64 MiB of HBM per device.

```python
import jax
import jax.numpy as jnp
from jax import lax

B = 128
STEPS = 2
NS_ITERS = 4
ROWS = 16384
NCOLS = 2048
N_BLK = 8


def levels(own_key, extent, cuts, least, largest):
    def one(dim, parts):
        draws = jax.random.uniform(jax.random.fold_in(jax.random.fold_in(own_key, 6), dim), (parts,), jnp.float32, least / len(cuts), largest / len(cuts))
        return jnp.repeat(jnp.exp(draws), extent[dim] // parts).reshape((-1,) + (1,) * (len(extent) - dim - 1))

    factor_of = one(*cuts[0])
    for cut in cuts[1:]:
        factor_of = factor_of * one(*cut)
    return factor_of


def bell_draw(stream_key, shape, spread, reach, split=(), kind=jnp.bfloat16):
    entries = jax.random.normal(stream_key, shape, jnp.float32) * spread
    if len(split) > 0:
        entries = levels(stream_key, shape, split, -0.22, 0.18) * entries
    return jnp.clip(entries, min=-reach, max=reach).astype(kind)


def setup_inputs(seed: int = 0) -> dict:
    streams_of = jax.random.split(jax.random.key(seed), 2)
    return {
        "matrix": bell_draw(streams_of[0], (ROWS, NCOLS), 1.0, 6.0, ((0, 4), (1, 8)), jnp.float32),
    }


HIGH = lax.Precision.HIGHEST

def inverse_root(square, bound_scale):
    identity = jnp.eye(square.shape[0], dtype=jnp.float32)
    current = square / bound_scale
    result = identity
    for count_index in range(NS_ITERS):
        factor = 1.5 * identity - 0.5 * jnp.dot(result, current, precision=HIGH)
        current = jnp.dot(current, factor, precision=HIGH)
        result = jnp.dot(factor, result, precision=HIGH)
    return result / jnp.sqrt(bound_scale)

def reference(matrix):
    blocks = matrix.reshape(ROWS, N_BLK, 2, B)
    left_block = blocks[:, :, 0]
    right_block = blocks[:, :, 1]
    identity = jnp.eye(B, dtype=jnp.float32)
    norm_list = []
    for step_index in range(STEPS):
        cross_gram = jnp.einsum('rpi,rpj->pij', left_block, right_block, precision=HIGH)
        first_norms = lax.optimization_barrier(jnp.sum(left_block * left_block, axis=0))
        second_norms = lax.optimization_barrier(jnp.sum(right_block * right_block, axis=0))
        cosines = cross_gram * lax.rsqrt(first_norms)[:, :, None] * lax.rsqrt(second_norms)[:, None, :]
        norm_list.append(jnp.mean(lax.optimization_barrier(jnp.sum(cosines * cosines, axis=(1, 2)))))
        coupling = 0.5 * cosines
        bound_scale = 1.0 + lax.optimization_barrier(jnp.sum(coupling * coupling, axis=(1, 2)))
        first_square = identity + jnp.einsum('pij,pkj->pik', coupling, coupling, precision=HIGH)
        second_square = identity + jnp.einsum('pji,pjk->pik', coupling, coupling, precision=HIGH)
        first_root = jax.vmap(inverse_root)(first_square, bound_scale)
        second_root = jax.vmap(inverse_root)(second_square, bound_scale)
        mixed_left = left_block - jnp.einsum('rpj,pij->rpi', right_block, coupling, precision=HIGH)
        mixed_right = right_block + jnp.einsum('rpi,pij->rpj', left_block, coupling, precision=HIGH)
        new_left = jnp.einsum('rpi,pij->rpj', mixed_left, first_root, precision=HIGH)
        new_right = jnp.einsum('rpi,pij->rpj', mixed_right, second_root, precision=HIGH)
        if step_index % 2 == 0:
            left_block = jnp.roll(new_left, 1, axis=1)
            right_block = new_right
        else:
            left_block = new_left
            right_block = jnp.roll(new_right, 1, axis=1)
    rotated = jnp.stack([left_block, right_block], axis=2).reshape(ROWS, 2 * B * N_BLK)
    return (rotated, jnp.stack(norm_list))
```

```python
import functools

import jax
import jax.numpy as jnp
from jax import lax
from jax.experimental import pallas as pl
from jax.experimental.pallas import tpu as pltpu
from jax.sharding import PartitionSpec as P

STEPS = 2
NS_ITERS = 4
MESH = pl.DeviceIdType.MESH
F32 = jnp.float32
BF16 = jnp.bfloat16


def split(value):
    high = value.astype(BF16)
    return high, (value - high.astype(F32)).astype(BF16)


def dot(a, b):
    return jnp.dot(a, b, preferred_element_type=F32)


def product(a, b):
    ah, al = split(a)
    bh, bl = split(b)
    width = b.shape[1]
    both = dot(
        jnp.concatenate([ah, al], axis=1),
        jnp.concatenate(
            [
                jnp.concatenate([bh, bl], axis=1),
                jnp.concatenate([bh, jnp.zeros_like(bl)], axis=1),
            ],
            axis=0,
        ),
    )
    return both[:, :width] + both[:, width:]


def mixing(cosines):
    width = cosines.shape[0]
    rows = lax.broadcasted_iota(jnp.int32, (width, width), 0)
    columns = lax.broadcasted_iota(jnp.int32, (width, width), 1)
    identity = jnp.where(rows == columns, 1.0, 0.0).astype(F32)
    coupling = 0.5 * cosines
    flipped = coupling.T
    scale = 1.0 + jnp.sum(coupling * coupling, keepdims=True)
    shrink = 1.0 / scale
    current = [
        (identity + product(coupling, flipped)) * shrink,
        (identity + product(flipped, coupling)) * shrink,
    ]
    result = [None, None]
    for count in range(NS_ITERS):
        for side in range(2):
            y, z = current[side], result[side]
            inner = y if z is None else product(z, y)
            factor = 1.5 * identity - 0.5 * inner
            if count < NS_ITERS - 1:
                current[side] = product(y, factor)
            result[side] = factor if z is None else product(factor, z)
    root = 1.0 / jnp.sqrt(scale)
    first, second = result[0] * root, result[1] * root
    return (
        jnp.concatenate([first, product(coupling, second)], axis=1),
        jnp.concatenate([-product(flipped, first), second], axis=1),
    )


def kernel(
    row_count, blk_count, chunk, gram_chunk,
    x_hbm, out_hbm, off_ref,
    xv, move0, stay0, come0, move1, stay1, acc, norms, gath, weights, measure, mgath,
    load_sem, send0, recv0, send1, recv1, out_sem, gsend, grecv, msend, mrecv,
):
    rows, both = x_hbm.shape
    width = both // 2
    chunks = rows // chunk
    row, blk = lax.axis_index("row"), lax.axis_index("blk")
    after = lax.rem(blk + 1, blk_count)

    barrier = pltpu.get_barrier_semaphore()
    for k in range(1, row_count):
        pl.semaphore_signal(
            barrier, inc=1, device_id={"row": lax.rem(row + k, row_count)}, device_id_type=MESH
        )

    def greet(k, carry):
        pl.semaphore_signal(
            barrier, inc=1, device_id={"blk": lax.rem(blk + k, blk_count)}, device_id_type=MESH
        )
        return carry

    lax.fori_loop(1, blk_count, greet, 0)

    def at(i, size):
        return pl.ds(pl.multiple_of(i * size, size), size)

    def load(i):
        return pltpu.make_async_copy(
            x_hbm.at[at(i, gram_chunk)], xv.at[at(i, gram_chunk)], load_sem.at[i]
        )

    def start_load(i, carry):
        load(i).start()
        return carry

    lax.fori_loop(0, rows // gram_chunk, start_load, 0)

    def add_gram(left, right):
        lh, ll = split(left)
        rh, rl = split(right)
        acc[...] += lax.dot_general(
            jnp.concatenate([lh, ll], axis=1),
            jnp.concatenate([rh, rl], axis=1),
            (((0,), (0,)), ((), ())),
            preferred_element_type=F32,
        )
        norms[0:8] += jnp.sum((left * left).reshape(-1, 8, width), axis=0)
        norms[8:16] += jnp.sum((right * right).reshape(-1, 8, width), axis=0)

    def clear():
        acc[...] = jnp.zeros_like(acc)
        norms[...] = jnp.zeros_like(norms)

    def exchange(step, peer_of):
        def copy(owner, peer, k):
            return pltpu.make_async_remote_copy(
                src_ref=gath.at[step, owner],
                dst_ref=gath.at[step, owner],
                send_sem=gsend.at[step, k],
                recv_sem=grecv.at[step, owner],
                device_id={"row": peer},
                device_id_type=MESH,
            )

        gath[step, row, 0:width] = (
            acc[:width, :width] + acc[:width, width:] + acc[width:, :width]
        ) + acc[width:, width:]
        first = jnp.sum(norms[0:8], axis=0, keepdims=True)
        second = jnp.sum(norms[8:16], axis=0, keepdims=True)
        gath[step, row, width:width + 8] = jnp.broadcast_to(first, (8, width))
        gath[step, row, width + 8:width + 16] = jnp.broadcast_to(second, (8, width))
        if step == 0:
            pl.semaphore_wait(barrier, row_count + blk_count - 2)
        for k in range(1, row_count):
            copy(row, lax.rem(row + k, row_count), k).start()
        for k in range(1, row_count):
            peer = lax.rem(row + k, row_count)
            copy(peer, peer, k).wait_recv()
        total = gath[step, 0]
        for r in range(1, row_count):
            total = total + gath[step, r]
        for k in range(1, row_count):
            copy(row, lax.rem(row + k, row_count), k).wait_send()
        cross = total[:width]
        first = lax.rsqrt(jnp.broadcast_to(total[width:width + 1], (width, width))).T
        second = lax.rsqrt(jnp.broadcast_to(total[width + 8:width + 9], (width, width)))
        cosines = cross * first * second
        measure[step:step + 1] = jnp.broadcast_to(
            jnp.sum(cosines * cosines, keepdims=True), (1, width)
        )
        top, bottom = mixing(cosines)
        high, low = split(top)
        weights[0, :width] = high
        weights[1, :width] = low
        high, low = split(bottom)
        weights[0, width:] = high
        weights[1, width:] = low

    def transform(left, right):
        lh, ll = split(left)
        rh, rl = split(right)
        high = jnp.concatenate([lh, rh], axis=1)
        low = jnp.concatenate([ll, rl], axis=1)
        return dot(high, weights[0]) + (dot(high, weights[1]) + dot(low, weights[0]))

    def first_move(i):
        return pltpu.make_async_remote_copy(
            src_ref=move0.at[at(i, chunk)], dst_ref=come0.at[at(i, chunk)],
            send_sem=send0.at[i], recv_sem=recv0.at[i],
            device_id={"blk": after}, device_id_type=MESH,
        )

    def second_move(i):
        return pltpu.make_async_remote_copy(
            src_ref=move1.at[at(i, chunk)], dst_ref=out_hbm.at[at(i, chunk), pl.ds(width, width)],
            send_sem=send1.at[i], recv_sem=recv1.at[i],
            device_id={"blk": after}, device_id_type=MESH,
        )

    def store(i):
        return pltpu.make_async_copy(
            stay1.at[at(i, chunk)], out_hbm.at[at(i, chunk), pl.ds(0, width)], out_sem.at[i]
        )

    def message(owner, peer):
        return pltpu.make_async_remote_copy(
            src_ref=mgath.at[owner], dst_ref=mgath.at[owner],
            send_sem=msend.at[peer], recv_sem=mrecv.at[owner],
            device_id={"blk": peer}, device_id_type=MESH,
        )

    clear()

    def gram0(i, carry):
        load(i).wait()
        part = at(i, gram_chunk)
        add_gram(xv[part, 0:width], xv[part, width:both])
        return carry

    lax.fori_loop(0, rows // gram_chunk, gram0, 0)
    measure[...] = jnp.zeros_like(measure)
    exchange(0, None)

    def turn0(i, carry):
        part = at(i, chunk)
        mixed = transform(xv[part, 0:width], xv[part, width:both])
        move0[part] = mixed[:, :width]
        stay0[part] = mixed[:, width:]

        @pl.when(i > 0)
        def _():
            first_move(i - 1).start()

        return carry

    lax.fori_loop(0, chunks, turn0, 0)
    first_move(chunks - 1).start()

    clear()

    def gram1(i, carry):
        first_move(i).wait_recv()
        part = at(i, chunk)
        add_gram(come0[part], stay0[part])
        return carry

    lax.fori_loop(0, chunks, gram1, 0)
    exchange(1, None)

    def turn1(i, carry):
        part = at(i, chunk)
        mixed = transform(come0[part], stay0[part])
        stay1[part] = mixed[:, :width]
        move1[part] = mixed[:, width:]

        @pl.when(i > 0)
        def _():
            second_move(i - 1).start()
            store(i - 1).start()

        return carry

    lax.fori_loop(0, chunks, turn1, 0)
    second_move(chunks - 1).start()
    store(chunks - 1).start()

    mgath[blk] = measure[...]

    def tell(k, carry):
        message(blk, lax.rem(blk + k, blk_count)).start()
        return carry

    lax.fori_loop(1, blk_count, tell, 0)

    def hear(k, carry):
        peer = lax.rem(blk + k, blk_count)
        message(peer, peer).wait_recv()
        return carry

    lax.fori_loop(1, blk_count, hear, 0)
    means = jnp.sum(mgath[...], axis=0) / float(blk_count)
    for step in range(STEPS):
        off_ref[step] = jnp.max(means[step:step + 1])

    def finish(i, carry):
        first_move(i).wait_send()
        store(i).wait()
        second_move(i).wait_send()
        second_move(i).wait_recv()
        return carry

    lax.fori_loop(0, chunks, finish, 0)

    def told(k, carry):
        message(blk, lax.rem(blk + k, blk_count)).wait_send()
        return carry

    lax.fori_loop(1, blk_count, told, 0)


def on_device(row_count, blk_count, matrix):
    rows, both = matrix.shape
    width = both // 2
    chunk = rows // 16
    gram_chunk = rows // 8
    dma = pltpu.SemaphoreType.DMA
    block = pltpu.VMEM((rows, width), F32)
    return pl.pallas_call(
        functools.partial(kernel, row_count, blk_count, chunk, gram_chunk),
        out_shape=(
            jax.ShapeDtypeStruct((rows, both), F32),
            jax.ShapeDtypeStruct((STEPS,), F32),
        ),
        in_specs=[pl.BlockSpec(memory_space=pl.ANY)],
        out_specs=(
            pl.BlockSpec(memory_space=pl.ANY),
            pl.BlockSpec(memory_space=pltpu.SMEM),
        ),
        scratch_shapes=[
            pltpu.VMEM((rows, both), F32),
            block, block, block, block, block,
            pltpu.VMEM((both, both), F32),
            pltpu.VMEM((16, width), F32),
            pltpu.VMEM((STEPS, row_count, width + 16, width), F32),
            pltpu.VMEM((2, both, both), BF16),
            pltpu.VMEM((8, width), F32),
            pltpu.VMEM((blk_count, 8, width), F32),
            dma((rows // gram_chunk,)),
            dma((16,)), dma((16,)), dma((16,)), dma((16,)), dma((16,)),
            dma((STEPS, row_count)), dma((STEPS, row_count)),
            dma((blk_count,)), dma((blk_count,)),
        ],
        compiler_params=pltpu.CompilerParams(
            collective_id=0, has_side_effects=True, vmem_limit_bytes=40 * 1024 * 1024
        ),
    )(matrix)


def solution(mesh):
    return jax.shard_map(
        functools.partial(on_device, mesh.shape["row"], mesh.shape["blk"]),
        mesh=mesh,
        in_specs=(P("row", "blk"),),
        out_specs=(P("row", "blk"), P()),
        check_vma=False,
    )
```

```python
import functools

import jax
import jax.numpy as jnp
from jax import lax
from jax.experimental import pallas as pl
from jax.experimental.pallas import tpu as pltpu
from jax.sharding import PartitionSpec as P

STEPS = 2
NS_ITERS = 4
MESH = pl.DeviceIdType.MESH
F32 = jnp.float32
BF16 = jnp.bfloat16


def split(value):
    high = value.astype(BF16)
    return high, (value - high.astype(F32)).astype(BF16)


def dot(a, b):
    return jnp.dot(a, b, preferred_element_type=F32)


def product(a, b):
    ah, al = split(a)
    bh, bl = split(b)
    width = b.shape[1]
    both = dot(
        jnp.concatenate([ah, al], axis=1),
        jnp.concatenate(
            [
                jnp.concatenate([bh, bl], axis=1),
                jnp.concatenate([bh, jnp.zeros_like(bl)], axis=1),
            ],
            axis=0,
        ),
    )
    return both[:, :width] + both[:, width:]


def mixing(cosines):
    width = cosines.shape[0]
    rows = lax.broadcasted_iota(jnp.int32, (width, width), 0)
    columns = lax.broadcasted_iota(jnp.int32, (width, width), 1)
    identity = jnp.where(rows == columns, 1.0, 0.0).astype(F32)
    coupling = 0.5 * cosines
    flipped = coupling.T
    scale = 1.0 + jnp.sum(coupling * coupling, keepdims=True)
    shrink = 1.0 / scale
    current = [
        (identity + product(coupling, flipped)) * shrink,
        (identity + product(flipped, coupling)) * shrink,
    ]
    result = [None, None]
    for count in range(NS_ITERS):
        for side in range(2):
            y, z = current[side], result[side]
            inner = y if z is None else product(z, y)
            factor = 1.5 * identity - 0.5 * inner
            if count < NS_ITERS - 1:
                current[side] = product(y, factor)
            result[side] = factor if z is None else product(factor, z)
    root = 1.0 / jnp.sqrt(scale)
    first, second = result[0] * root, result[1] * root
    return (
        jnp.concatenate([first, product(coupling, second)], axis=1),
        jnp.concatenate([-product(flipped, first), second], axis=1),
    )


def kernel(
    row_count, blk_count, chunk, gram_chunk, early,
    x_hbm, out_ref, off_ref,
    xv, move0, stay0, come0, move1, raw, rest, skip,
    acc, norms, gath, weights, coses, cosin, measure, mgath,
    load_sem, send0, recv0, send1, recv1, gsend, grecv, msend, mrecv, esend, erecv,
):
    rows, both = x_hbm.shape
    width = both // 2
    chunks = rows // chunk
    row, blk = lax.axis_index("row"), lax.axis_index("blk")
    after = lax.rem(blk + 1, blk_count)
    second = lax.rem(blk + 2, blk_count)
    early_rows = pl.ds(0, early * chunk)

    barrier = pltpu.get_barrier_semaphore()
    for k in range(1, row_count):
        pl.semaphore_signal(
            barrier, inc=1, device_id={"row": lax.rem(row + k, row_count)}, device_id_type=MESH
        )

    def greet(k, carry):
        pl.semaphore_signal(
            barrier, inc=1, device_id={"blk": lax.rem(blk + k, blk_count)}, device_id_type=MESH
        )
        return carry

    lax.fori_loop(1, blk_count, greet, 0)

    def at(i, size):
        return pl.ds(pl.multiple_of(i * size, size), size)

    def load(i):
        return pltpu.make_async_copy(
            x_hbm.at[at(i, gram_chunk)], xv.at[at(i, gram_chunk)], load_sem.at[i]
        )

    def start_load(i, carry):
        load(i).start()
        return carry

    lax.fori_loop(0, rows // gram_chunk, start_load, 0)

    def ahead(source, target, k, peer):
        return pltpu.make_async_remote_copy(
            src_ref=source, dst_ref=target, send_sem=esend.at[k], recv_sem=erecv.at[k],
            device_id={"blk": peer}, device_id_type=MESH,
        )

    raw_move = ahead(x_hbm.at[early_rows], raw, 0, after)
    skip_move = ahead(move0.at[early_rows], skip, 1, second)
    cos_moves = [ahead(coses.at[s], cosin.at[s], 2 + s, after) for s in range(STEPS)]

    pl.semaphore_wait(barrier, row_count + blk_count - 2)
    raw_move.start()

    def add_gram(left, right):
        lh, ll = split(left)
        rh, rl = split(right)
        acc[...] += lax.dot_general(
            jnp.concatenate([lh, ll], axis=1),
            jnp.concatenate([rh, rl], axis=1),
            (((0,), (0,)), ((), ())),
            preferred_element_type=F32,
        )
        norms[0:8] += jnp.sum((left * left).reshape(-1, 8, width), axis=0)
        norms[8:16] += jnp.sum((right * right).reshape(-1, 8, width), axis=0)

    def clear():
        acc[...] = jnp.zeros_like(acc)
        norms[...] = jnp.zeros_like(norms)

    def mix(slot, cosines):
        top, bottom = mixing(cosines)
        high, low = split(top)
        weights[slot, 0, :width] = high
        weights[slot, 1, :width] = low
        high, low = split(bottom)
        weights[slot, 0, width:] = high
        weights[slot, 1, width:] = low

    def exchange(step):
        def copy(owner, peer, k):
            return pltpu.make_async_remote_copy(
                src_ref=gath.at[step, owner],
                dst_ref=gath.at[step, owner],
                send_sem=gsend.at[step, k],
                recv_sem=grecv.at[step, owner],
                device_id={"row": peer},
                device_id_type=MESH,
            )

        gath[step, row, 0:width] = (
            acc[:width, :width] + acc[:width, width:] + acc[width:, :width]
        ) + acc[width:, width:]
        first = jnp.sum(norms[0:8], axis=0, keepdims=True)
        second = jnp.sum(norms[8:16], axis=0, keepdims=True)
        gath[step, row, width:width + 8] = jnp.broadcast_to(first, (8, width))
        gath[step, row, width + 8:width + 16] = jnp.broadcast_to(second, (8, width))
        for k in range(1, row_count):
            copy(row, lax.rem(row + k, row_count), k).start()
        for k in range(1, row_count):
            peer = lax.rem(row + k, row_count)
            copy(peer, peer, k).wait_recv()
        total = gath[step, 0]
        for r in range(1, row_count):
            total = total + gath[step, r]
        for k in range(1, row_count):
            copy(row, lax.rem(row + k, row_count), k).wait_send()
        cross = total[:width]
        first = lax.rsqrt(jnp.broadcast_to(total[width:width + 1], (width, width))).T
        second = lax.rsqrt(jnp.broadcast_to(total[width + 8:width + 9], (width, width)))
        cosines = cross * first * second
        measure[step:step + 1] = jnp.broadcast_to(
            jnp.sum(cosines * cosines, keepdims=True), (1, width)
        )
        coses[step] = cosines
        mix(0, cosines)
        cos_moves[step].start()

    def transform(slot, left, right):
        lh, ll = split(left)
        rh, rl = split(right)
        high = jnp.concatenate([lh, rh], axis=1)
        low = jnp.concatenate([ll, rl], axis=1)
        own, fine = weights[slot, 0], weights[slot, 1]
        return dot(high, own) + (dot(high, fine) + dot(low, own))

    def first_move(i):
        return pltpu.make_async_remote_copy(
            src_ref=move0.at[at(i, chunk)], dst_ref=come0.at[at(i, chunk)],
            send_sem=send0.at[i], recv_sem=recv0.at[i],
            device_id={"blk": after}, device_id_type=MESH,
        )

    def second_move(i):
        return pltpu.make_async_remote_copy(
            src_ref=move1.at[at(i, chunk)], dst_ref=out_ref.at[at(i, chunk), pl.ds(width, width)],
            send_sem=send1.at[i], recv_sem=recv1.at[i],
            device_id={"blk": after}, device_id_type=MESH,
        )

    def message(owner, peer):
        return pltpu.make_async_remote_copy(
            src_ref=mgath.at[owner], dst_ref=mgath.at[owner],
            send_sem=msend.at[peer], recv_sem=mrecv.at[owner],
            device_id={"blk": peer}, device_id_type=MESH,
        )

    clear()

    def gram0(i, carry):
        load(i).wait()
        part = at(i, gram_chunk)
        add_gram(xv[part, 0:width], xv[part, width:both])
        return carry

    lax.fori_loop(0, rows // gram_chunk, gram0, 0)
    measure[...] = jnp.zeros_like(measure)
    exchange(0)

    def turn0(i, carry):
        part = at(i, chunk)
        mixed = transform(0, xv[part, 0:width], xv[part, width:both])
        move0[part] = mixed[:, :width]
        stay0[part] = mixed[:, width:]

        @pl.when(i > early)
        def _():
            first_move(i - 1).start()

        return carry

    lax.fori_loop(early, chunks, turn0, 0)
    first_move(chunks - 1).start()

    def own0(i, carry):
        part = at(i, chunk)
        mixed = transform(0, xv[part, 0:width], xv[part, width:both])
        move0[part] = mixed[:, :width]
        stay0[part] = mixed[:, width:]
        return carry

    lax.fori_loop(0, early, own0, 0)

    cos_moves[0].wait_recv()
    mix(1, cosin[0])
    raw_move.wait_recv()
    clear()

    def early0(i, carry):
        part = at(i, chunk)
        mixed = transform(1, raw[part, 0:width], raw[part, width:both])
        come0[part] = mixed[:, :width]
        rest[part] = mixed[:, width:]
        add_gram(mixed[:, :width], stay0[part])
        return carry

    lax.fori_loop(0, early, early0, 0)

    def gram1(i, carry):
        first_move(i).wait_recv()
        part = at(i, chunk)
        add_gram(come0[part], stay0[part])
        return carry

    lax.fori_loop(early, chunks, gram1, 0)
    skip_move.start()
    exchange(1)

    def turn1(i, carry):
        part = at(i, chunk)
        mixed = transform(0, come0[part], stay0[part])
        out_ref[part, 0:width] = mixed[:, :width]
        move1[part] = mixed[:, width:]

        @pl.when(i > early)
        def _():
            second_move(i - 1).start()

        return carry

    lax.fori_loop(early, chunks, turn1, 0)
    second_move(chunks - 1).start()

    def own1(i, carry):
        part = at(i, chunk)
        out_ref[part, 0:width] = transform(0, come0[part], stay0[part])[:, :width]
        return carry

    lax.fori_loop(0, early, own1, 0)
    cos_moves[1].wait_recv()
    mix(1, cosin[1])
    skip_move.wait_recv()

    def early1(i, carry):
        part = at(i, chunk)
        out_ref[part, width:both] = transform(1, skip[part], rest[part])[:, width:]
        return carry

    lax.fori_loop(0, early, early1, 0)

    mgath[blk] = measure[...]

    def tell(k, carry):
        message(blk, lax.rem(blk + k, blk_count)).start()
        return carry

    lax.fori_loop(1, blk_count, tell, 0)

    def hear(k, carry):
        peer = lax.rem(blk + k, blk_count)
        message(peer, peer).wait_recv()
        return carry

    lax.fori_loop(1, blk_count, hear, 0)
    means = jnp.sum(mgath[...], axis=0) / float(blk_count)
    for step in range(STEPS):
        off_ref[step] = jnp.max(means[step:step + 1])

    def finish(i, carry):
        first_move(i).wait_send()
        second_move(i).wait_send()
        second_move(i).wait_recv()
        return carry

    lax.fori_loop(early, chunks, finish, 0)
    raw_move.wait_send()
    skip_move.wait_send()
    for cos_move in cos_moves:
        cos_move.wait_send()

    def told(k, carry):
        message(blk, lax.rem(blk + k, blk_count)).wait_send()
        return carry

    lax.fori_loop(1, blk_count, told, 0)


def on_device(row_count, blk_count, matrix):
    rows, both = matrix.shape
    width = both // 2
    chunks, early = 16, 2
    chunk = rows // chunks
    gram_chunk = rows // 8
    dma = pltpu.SemaphoreType.DMA
    block = pltpu.VMEM((rows, width), F32)
    some = pltpu.VMEM((early * chunk, width), F32)
    return pl.pallas_call(
        functools.partial(kernel, row_count, blk_count, chunk, gram_chunk, early),
        out_shape=(
            jax.ShapeDtypeStruct((rows, both), F32),
            jax.ShapeDtypeStruct((STEPS,), F32),
        ),
        in_specs=[pl.BlockSpec(memory_space=pltpu.HBM)],
        out_specs=(
            pl.BlockSpec(memory_space=pltpu.VMEM),
            pl.BlockSpec(memory_space=pltpu.SMEM),
        ),
        scratch_shapes=[
            pltpu.VMEM((rows, both), F32),
            block, block, block, block,
            pltpu.VMEM((early * chunk, both), F32),
            some, some,
            pltpu.VMEM((both, both), F32),
            pltpu.VMEM((16, width), F32),
            pltpu.VMEM((STEPS, row_count, width + 16, width), F32),
            pltpu.VMEM((2, 2, both, both), BF16),
            pltpu.VMEM((STEPS, width, width), F32),
            pltpu.VMEM((STEPS, width, width), F32),
            pltpu.VMEM((8, width), F32),
            pltpu.VMEM((blk_count, 8, width), F32),
            dma((rows // gram_chunk,)),
            dma((chunks,)), dma((chunks,)), dma((chunks,)), dma((chunks,)),
            dma((STEPS, row_count)), dma((STEPS, row_count)),
            dma((blk_count,)), dma((blk_count,)),
            dma((2 + STEPS,)), dma((2 + STEPS,)),
        ],
        compiler_params=pltpu.CompilerParams(
            collective_id=0, has_side_effects=True, vmem_limit_bytes=40 * 1024 * 1024
        ),
    )(matrix)


def solution(mesh):
    return jax.shard_map(
        functools.partial(on_device, mesh.shape["row"], mesh.shape["blk"]),
        mesh=mesh,
        in_specs=(P("row", "blk"),),
        out_specs=(P("row", "blk"), P()),
        check_vma=False,
    )
```

```python
import functools

import jax
import jax.numpy as jnp
from jax import lax
from jax.experimental import pallas as pl
from jax.experimental.pallas import tpu as pltpu
from jax.sharding import PartitionSpec as P

STEPS = 2
NS_ITERS = 4
MESH = pl.DeviceIdType.MESH
F32 = jnp.float32
BF16 = jnp.bfloat16


def split(value):
    high = value.astype(BF16)
    return high, (value - high.astype(F32)).astype(BF16)


def dot(a, b):
    return jnp.dot(a, b, preferred_element_type=F32)


def product(a, b):
    ah, al = split(a)
    bh, bl = split(b)
    width = b.shape[1]
    both = dot(
        jnp.concatenate([ah, al], axis=1),
        jnp.concatenate(
            [
                jnp.concatenate([bh, bl], axis=1),
                jnp.concatenate([bh, jnp.zeros_like(bl)], axis=1),
            ],
            axis=0,
        ),
    )
    return both[:, :width] + both[:, width:]


def mixing(cosines):
    width = cosines.shape[0]
    rows = lax.broadcasted_iota(jnp.int32, (width, width), 0)
    columns = lax.broadcasted_iota(jnp.int32, (width, width), 1)
    identity = jnp.where(rows == columns, 1.0, 0.0).astype(F32)
    coupling = 0.5 * cosines
    flipped = coupling.T
    scale = 1.0 + jnp.sum(coupling * coupling, keepdims=True)
    shrink = 1.0 / scale
    current = [
        (identity + product(coupling, flipped)) * shrink,
        (identity + product(flipped, coupling)) * shrink,
    ]
    result = [None, None]
    for count in range(NS_ITERS):
        for side in range(2):
            y, z = current[side], result[side]
            inner = y if z is None else product(z, y)
            factor = 1.5 * identity - 0.5 * inner
            if count < NS_ITERS - 1:
                current[side] = product(y, factor)
            result[side] = factor if z is None else product(factor, z)
    root = 1.0 / jnp.sqrt(scale)
    first, second = result[0] * root, result[1] * root
    return (
        jnp.concatenate([first, product(coupling, second)], axis=1),
        jnp.concatenate([-product(flipped, first), second], axis=1),
    )


def kernel(
    row_count, blk_count, chunk, gram_chunk, early,
    x_hbm, out_ref, off_ref,
    xv, move0, stay0, come0, move1, raw, rest, skip,
    acc, norms, gath, weights, coses, cosin, measure, mgath,
    load_sem, send0, recv0, send1, recv1, gsend, grecv, msend, mrecv, esend, erecv,
):
    rows, both = x_hbm.shape
    width = both // 2
    chunks = rows // chunk
    row, blk = lax.axis_index("row"), lax.axis_index("blk")
    after = lax.rem(blk + 1, blk_count)
    second = lax.rem(blk + 2, blk_count)
    early_rows = pl.ds(0, early * chunk)

    barrier = pltpu.get_barrier_semaphore()
    for k in range(1, row_count):
        pl.semaphore_signal(
            barrier, inc=1, device_id={"row": lax.rem(row + k, row_count)}, device_id_type=MESH
        )

    def greet(k, carry):
        pl.semaphore_signal(
            barrier, inc=1, device_id={"blk": lax.rem(blk + k, blk_count)}, device_id_type=MESH
        )
        return carry

    lax.fori_loop(1, blk_count, greet, 0)

    def at(i, size):
        return pl.ds(pl.multiple_of(i * size, size), size)

    def load(i):
        return pltpu.make_async_copy(
            x_hbm.at[at(i, gram_chunk)], xv.at[at(i, gram_chunk)], load_sem.at[i]
        )

    def start_load(i, carry):
        load(i).start()
        return carry

    lax.fori_loop(0, rows // gram_chunk, start_load, 0)

    def ahead(source, target, k, peer):
        return pltpu.make_async_remote_copy(
            src_ref=source, dst_ref=target, send_sem=esend.at[k], recv_sem=erecv.at[k],
            device_id={"blk": peer}, device_id_type=MESH,
        )

    raw_move = ahead(x_hbm.at[early_rows], raw, 0, after)
    skip_move = ahead(move0.at[early_rows], skip, 1, second)
    cos_moves = [ahead(coses.at[s], cosin.at[s], 2 + s, after) for s in range(STEPS)]

    pl.semaphore_wait(barrier, row_count + blk_count - 2)
    raw_move.start()

    def add_gram(left, right):
        lh, ll = split(left)
        rh, rl = split(right)
        acc[...] += lax.dot_general(
            jnp.concatenate([lh, ll], axis=1),
            jnp.concatenate([rh, rl], axis=1),
            (((0,), (0,)), ((), ())),
            preferred_element_type=F32,
        )
        norms[0:8] += jnp.sum((left * left).reshape(-1, 8, width), axis=0)
        norms[8:16] += jnp.sum((right * right).reshape(-1, 8, width), axis=0)

    def clear():
        acc[...] = jnp.zeros_like(acc)
        norms[...] = jnp.zeros_like(norms)

    def mix(slot, cosines):
        top, bottom = mixing(cosines)
        high, low = split(top)
        weights[slot, 0, :width] = high
        weights[slot, 1, :width] = low
        high, low = split(bottom)
        weights[slot, 0, width:] = high
        weights[slot, 1, width:] = low

    def exchange(step):
        def copy(owner, peer, k):
            return pltpu.make_async_remote_copy(
                src_ref=gath.at[step, owner],
                dst_ref=gath.at[step, owner],
                send_sem=gsend.at[step, k],
                recv_sem=grecv.at[step, owner],
                device_id={"row": peer},
                device_id_type=MESH,
            )

        gath[step, row, 0:width] = (
            acc[:width, :width] + acc[:width, width:] + acc[width:, :width]
        ) + acc[width:, width:]
        first = jnp.sum(norms[0:8], axis=0, keepdims=True)
        second = jnp.sum(norms[8:16], axis=0, keepdims=True)
        gath[step, row, width:width + 8] = jnp.broadcast_to(first, (8, width))
        gath[step, row, width + 8:width + 16] = jnp.broadcast_to(second, (8, width))
        for k in range(1, row_count):
            copy(row, lax.rem(row + k, row_count), k).start()
        for k in range(1, row_count):
            peer = lax.rem(row + k, row_count)
            copy(peer, peer, k).wait_recv()
        total = gath[step, 0]
        for r in range(1, row_count):
            total = total + gath[step, r]
        for k in range(1, row_count):
            copy(row, lax.rem(row + k, row_count), k).wait_send()
        cross = total[:width]
        first = lax.rsqrt(jnp.broadcast_to(total[width:width + 1], (width, width))).T
        second = lax.rsqrt(jnp.broadcast_to(total[width + 8:width + 9], (width, width)))
        cosines = cross * first * second
        measure[step:step + 1] = jnp.broadcast_to(
            jnp.sum(cosines * cosines, keepdims=True), (1, width)
        )
        coses[step] = cosines
        mix(0, cosines)
        cos_moves[step].start()

    def transform(slot, left, right):
        lh, ll = split(left)
        rh, rl = split(right)
        high = jnp.concatenate([lh, rh], axis=1)
        low = jnp.concatenate([ll, rl], axis=1)
        own, fine = weights[slot, 0], weights[slot, 1]
        return dot(high, own) + (dot(high, fine) + dot(low, own))

    def first_move(i):
        return pltpu.make_async_remote_copy(
            src_ref=move0.at[at(i, chunk)], dst_ref=come0.at[at(i, chunk)],
            send_sem=send0.at[i], recv_sem=recv0.at[i],
            device_id={"blk": after}, device_id_type=MESH,
        )

    def second_move(i):
        return pltpu.make_async_remote_copy(
            src_ref=move1.at[at(i, chunk)], dst_ref=out_ref.at[at(i, chunk), pl.ds(width, width)],
            send_sem=send1.at[i], recv_sem=recv1.at[i],
            device_id={"blk": after}, device_id_type=MESH,
        )

    def message(owner, peer):
        return pltpu.make_async_remote_copy(
            src_ref=mgath.at[owner], dst_ref=mgath.at[owner],
            send_sem=msend.at[peer], recv_sem=mrecv.at[owner],
            device_id={"blk": peer}, device_id_type=MESH,
        )

    clear()

    def gram0(i, carry):
        load(i).wait()
        part = at(i, gram_chunk)
        add_gram(xv[part, 0:width], xv[part, width:both])
        return carry

    lax.fori_loop(0, rows // gram_chunk, gram0, 0)
    measure[...] = jnp.zeros_like(measure)
    exchange(0)

    def turn0(i, carry):
        part = at(i, chunk)
        mixed = transform(0, xv[part, 0:width], xv[part, width:both])
        move0[part] = mixed[:, :width]
        stay0[part] = mixed[:, width:]

        @pl.when(i > early)
        def _():
            first_move(i - 1).start()

        return carry

    lax.fori_loop(early, chunks, turn0, 0)
    first_move(chunks - 1).start()

    def own0(i, carry):
        part = at(i, chunk)
        mixed = transform(0, xv[part, 0:width], xv[part, width:both])
        move0[part] = mixed[:, :width]
        stay0[part] = mixed[:, width:]
        return carry

    lax.fori_loop(0, early, own0, 0)

    cos_moves[0].wait_recv()
    mix(1, cosin[0])
    raw_move.wait_recv()
    clear()

    def early0(i, carry):
        part = at(i, chunk)
        mixed = transform(1, raw[part, 0:width], raw[part, width:both])
        come0[part] = mixed[:, :width]
        rest[part] = mixed[:, width:]
        add_gram(mixed[:, :width], stay0[part])
        return carry

    lax.fori_loop(0, early, early0, 0)

    def gram1(i, carry):
        first_move(i).wait_recv()
        part = at(i, chunk)
        add_gram(come0[part], stay0[part])
        return carry

    lax.fori_loop(early, chunks, gram1, 0)
    skip_move.start()
    exchange(1)

    def turn1(i, carry):
        part = at(i, chunk)
        mixed = transform(0, come0[part], stay0[part])
        out_ref[part, 0:width] = mixed[:, :width]
        move1[part] = mixed[:, width:]

        @pl.when(i > early)
        def _():
            second_move(i - 1).start()

        return carry

    lax.fori_loop(early, chunks, turn1, 0)
    second_move(chunks - 1).start()

    def own1(i, carry):
        part = at(i, chunk)
        out_ref[part, 0:width] = transform(0, come0[part], stay0[part])[:, :width]
        return carry

    lax.fori_loop(0, early, own1, 0)
    cos_moves[1].wait_recv()
    mix(1, cosin[1])
    skip_move.wait_recv()

    def early1(i, carry):
        part = at(i, chunk)
        out_ref[part, width:both] = transform(1, skip[part], rest[part])[:, width:]
        return carry

    lax.fori_loop(0, early, early1, 0)

    mgath[blk] = measure[...]

    def tell(k, carry):
        message(blk, lax.rem(blk + k, blk_count)).start()
        return carry

    lax.fori_loop(1, blk_count, tell, 0)

    def hear(k, carry):
        peer = lax.rem(blk + k, blk_count)
        message(peer, peer).wait_recv()
        return carry

    lax.fori_loop(1, blk_count, hear, 0)
    means = jnp.sum(mgath[...], axis=0) / float(blk_count)
    for step in range(STEPS):
        off_ref[step] = jnp.max(means[step:step + 1])

    def finish(i, carry):
        first_move(i).wait_send()
        second_move(i).wait_send()
        second_move(i).wait_recv()
        return carry

    lax.fori_loop(early, chunks, finish, 0)
    raw_move.wait_send()
    skip_move.wait_send()
    for cos_move in cos_moves:
        cos_move.wait_send()

    def told(k, carry):
        message(blk, lax.rem(blk + k, blk_count)).wait_send()
        return carry

    lax.fori_loop(1, blk_count, told, 0)


def on_device(row_count, blk_count, matrix):
    rows, both = matrix.shape
    width = both // 2
    chunks, early = 16, 3
    chunk = rows // chunks
    gram_chunk = rows // 8
    dma = pltpu.SemaphoreType.DMA
    block = pltpu.VMEM((rows, width), F32)
    some = pltpu.VMEM((early * chunk, width), F32)
    return pl.pallas_call(
        functools.partial(kernel, row_count, blk_count, chunk, gram_chunk, early),
        out_shape=(
            jax.ShapeDtypeStruct((rows, both), F32),
            jax.ShapeDtypeStruct((STEPS,), F32),
        ),
        in_specs=[pl.BlockSpec(memory_space=pltpu.HBM)],
        out_specs=(
            pl.BlockSpec(memory_space=pltpu.VMEM),
            pl.BlockSpec(memory_space=pltpu.SMEM),
        ),
        scratch_shapes=[
            pltpu.VMEM((rows, both), F32),
            block, block, block, block,
            pltpu.VMEM((early * chunk, both), F32),
            some, some,
            pltpu.VMEM((both, both), F32),
            pltpu.VMEM((16, width), F32),
            pltpu.VMEM((STEPS, row_count, width + 16, width), F32),
            pltpu.VMEM((2, 2, both, both), BF16),
            pltpu.VMEM((STEPS, width, width), F32),
            pltpu.VMEM((STEPS, width, width), F32),
            pltpu.VMEM((8, width), F32),
            pltpu.VMEM((blk_count, 8, width), F32),
            dma((rows // gram_chunk,)),
            dma((chunks,)), dma((chunks,)), dma((chunks,)), dma((chunks,)),
            dma((STEPS, row_count)), dma((STEPS, row_count)),
            dma((blk_count,)), dma((blk_count,)),
            dma((2 + STEPS,)), dma((2 + STEPS,)),
        ],
        compiler_params=pltpu.CompilerParams(
            collective_id=0, has_side_effects=True, vmem_limit_bytes=48 * 1024 * 1024
        ),
    )(matrix)


def solution(mesh):
    return jax.shard_map(
        functools.partial(on_device, mesh.shape["row"], mesh.shape["blk"]),
        mesh=mesh,
        in_specs=(P("row", "blk"),),
        out_specs=(P("row", "blk"), P()),
        check_vma=False,
    )
```

```python
import functools

import jax
import jax.numpy as jnp
from jax import lax
from jax.experimental import pallas as pl
from jax.experimental.pallas import tpu as pltpu
from jax.sharding import PartitionSpec as P

STEPS = 2
NS_ITERS = 4
MESH = pl.DeviceIdType.MESH
F32 = jnp.float32
BF16 = jnp.bfloat16


def split(value):
    high = value.astype(BF16)
    return high, (value - high.astype(F32)).astype(BF16)


def dot(a, b):
    return jnp.dot(a, b, preferred_element_type=F32)


def product(a, b):
    ah, al = split(a)
    bh, bl = split(b)
    width = b.shape[1]
    both = dot(
        jnp.concatenate([ah, al], axis=1),
        jnp.concatenate(
            [
                jnp.concatenate([bh, bl], axis=1),
                jnp.concatenate([bh, jnp.zeros_like(bl)], axis=1),
            ],
            axis=0,
        ),
    )
    return both[:, :width] + both[:, width:]


def mixing(cosines):
    width = cosines.shape[0]
    rows = lax.broadcasted_iota(jnp.int32, (width, width), 0)
    columns = lax.broadcasted_iota(jnp.int32, (width, width), 1)
    identity = jnp.where(rows == columns, 1.0, 0.0).astype(F32)
    coupling = 0.5 * cosines
    flipped = coupling.T
    scale = 1.0 + jnp.sum(coupling * coupling, keepdims=True)
    shrink = 1.0 / scale
    current = [
        (identity + product(coupling, flipped)) * shrink,
        (identity + product(flipped, coupling)) * shrink,
    ]
    result = [None, None]
    for count in range(NS_ITERS):
        for side in range(2):
            y, z = current[side], result[side]
            inner = y if z is None else product(z, y)
            factor = 1.5 * identity - 0.5 * inner
            if count < NS_ITERS - 1:
                current[side] = product(y, factor)
            result[side] = factor if z is None else product(factor, z)
    root = 1.0 / jnp.sqrt(scale)
    first, second = result[0] * root, result[1] * root
    return (
        jnp.concatenate([first, product(coupling, second)], axis=1),
        jnp.concatenate([-product(flipped, first), second], axis=1),
    )


def kernel(
    row_count, blk_count, chunk, gram_chunk, early, given,
    x_hbm, out_ref, off_ref,
    xv, move0, stay0, come0, move1, raw, rest, skip, hold,
    acc, norms, gath, weights, coses, cosin, measure, mgath,
    load_sem, send0, recv0, send1, recv1, gsend, grecv, msend, mrecv, esend, erecv,
):
    rows, both = x_hbm.shape
    width = both // 2
    chunks = rows // chunk
    row, blk = lax.axis_index("row"), lax.axis_index("blk")
    after = lax.rem(blk + 1, blk_count)
    second = lax.rem(blk + 2, blk_count)
    odd = lax.rem(blk, 2) == 1
    below = lax.rem(blk + blk_count - 1, blk_count)
    early_rows = pl.ds(0, early * chunk)
    given_rows = pl.ds(early * chunk, (given - early) * chunk)

    barrier = pltpu.get_barrier_semaphore()
    for k in range(1, row_count):
        pl.semaphore_signal(
            barrier, inc=1, device_id={"row": lax.rem(row + k, row_count)}, device_id_type=MESH
        )

    def greet(k, carry):
        pl.semaphore_signal(
            barrier, inc=1, device_id={"blk": lax.rem(blk + k, blk_count)}, device_id_type=MESH
        )
        return carry

    lax.fori_loop(1, blk_count, greet, 0)

    def at(i, size):
        return pl.ds(pl.multiple_of(i * size, size), size)

    def load(i):
        return pltpu.make_async_copy(
            x_hbm.at[at(i, gram_chunk)], xv.at[at(i, gram_chunk)], load_sem.at[i]
        )

    def start_load(i, carry):
        load(i).start()
        return carry

    lax.fori_loop(0, rows // gram_chunk, start_load, 0)

    def ahead(source, target, k, peer, sender=None):
        sender = k if sender is None else sender
        return pltpu.make_async_remote_copy(
            src_ref=source, dst_ref=target, send_sem=esend.at[sender], recv_sem=erecv.at[k],
            device_id={"blk": peer}, device_id_type=MESH,
        )

    raw_move = ahead(x_hbm.at[early_rows], raw, 0, after)
    skip_move = ahead(move0.at[pl.ds(0, given * chunk)], skip, 1, second)
    give_move = ahead(stay0.at[given_rows], rest.at[given_rows], 2 + STEPS, after)
    hold_move = ahead(stay0.at[given_rows], hold, 3 + STEPS, below)
    pass_move = ahead(hold, rest.at[given_rows], 2 + STEPS, second, 4 + STEPS)
    cos_moves = [ahead(coses.at[s], cosin.at[s], 2 + s, after) for s in range(STEPS)]

    pl.semaphore_wait(barrier, row_count + blk_count - 2)
    raw_move.start()

    def add_gram(left, right):
        lh, ll = split(left)
        rh, rl = split(right)
        acc[...] += lax.dot_general(
            jnp.concatenate([lh, ll], axis=1),
            jnp.concatenate([rh, rl], axis=1),
            (((0,), (0,)), ((), ())),
            preferred_element_type=F32,
        )
        norms[0:8] += jnp.sum((left * left).reshape(-1, 8, width), axis=0)
        norms[8:16] += jnp.sum((right * right).reshape(-1, 8, width), axis=0)

    def clear():
        acc[...] = jnp.zeros_like(acc)
        norms[...] = jnp.zeros_like(norms)

    def mix(slot, cosines):
        top, bottom = mixing(cosines)
        high, low = split(top)
        weights[slot, 0, :width] = high
        weights[slot, 1, :width] = low
        high, low = split(bottom)
        weights[slot, 0, width:] = high
        weights[slot, 1, width:] = low

    def exchange(step):
        def copy(owner, peer, k):
            return pltpu.make_async_remote_copy(
                src_ref=gath.at[step, owner],
                dst_ref=gath.at[step, owner],
                send_sem=gsend.at[step, k],
                recv_sem=grecv.at[step, owner],
                device_id={"row": peer},
                device_id_type=MESH,
            )

        gath[step, row, 0:width] = (
            acc[:width, :width] + acc[:width, width:] + acc[width:, :width]
        ) + acc[width:, width:]
        first = jnp.sum(norms[0:8], axis=0, keepdims=True)
        second = jnp.sum(norms[8:16], axis=0, keepdims=True)
        gath[step, row, width:width + 8] = jnp.broadcast_to(first, (8, width))
        gath[step, row, width + 8:width + 16] = jnp.broadcast_to(second, (8, width))
        for k in range(1, row_count):
            copy(row, lax.rem(row + k, row_count), k).start()
        for k in range(1, row_count):
            peer = lax.rem(row + k, row_count)
            copy(peer, peer, k).wait_recv()
        total = gath[step, 0]
        for r in range(1, row_count):
            total = total + gath[step, r]
        for k in range(1, row_count):
            copy(row, lax.rem(row + k, row_count), k).wait_send()
        cross = total[:width]
        first = lax.rsqrt(jnp.broadcast_to(total[width:width + 1], (width, width))).T
        second = lax.rsqrt(jnp.broadcast_to(total[width + 8:width + 9], (width, width)))
        cosines = cross * first * second
        measure[step:step + 1] = jnp.broadcast_to(
            jnp.sum(cosines * cosines, keepdims=True), (1, width)
        )
        coses[step] = cosines
        cos_moves[step].start()
        mix(0, cosines)

    def transform(slot, left, right):
        lh, ll = split(left)
        rh, rl = split(right)
        high = jnp.concatenate([lh, rh], axis=1)
        low = jnp.concatenate([ll, rl], axis=1)
        own, fine = weights[slot, 0], weights[slot, 1]
        return dot(high, own) + (dot(high, fine) + dot(low, own))

    def first_move(i):
        return pltpu.make_async_remote_copy(
            src_ref=move0.at[at(i, chunk)], dst_ref=come0.at[at(i, chunk)],
            send_sem=send0.at[i], recv_sem=recv0.at[i],
            device_id={"blk": after}, device_id_type=MESH,
        )

    def second_move(i):
        return pltpu.make_async_remote_copy(
            src_ref=move1.at[at(i, chunk)], dst_ref=out_ref.at[at(i, chunk), pl.ds(width, width)],
            send_sem=send1.at[i], recv_sem=recv1.at[i],
            device_id={"blk": after}, device_id_type=MESH,
        )

    def message(owner, peer):
        return pltpu.make_async_remote_copy(
            src_ref=mgath.at[owner], dst_ref=mgath.at[owner],
            send_sem=msend.at[peer], recv_sem=mrecv.at[owner],
            device_id={"blk": peer}, device_id_type=MESH,
        )

    clear()

    def gram0(i, carry):
        load(i).wait()
        part = at(i, gram_chunk)
        add_gram(xv[part, 0:width], xv[part, width:both])
        return carry

    lax.fori_loop(0, rows // gram_chunk, gram0, 0)
    measure[...] = jnp.zeros_like(measure)
    exchange(0)

    def turn0(i, carry):
        part = at(i, chunk)
        mixed = transform(0, xv[part, 0:width], xv[part, width:both])
        move0[part] = mixed[:, :width]
        stay0[part] = mixed[:, width:]

        @pl.when(i > early)
        def _():
            first_move(i - 1).start()

        return carry

    lax.fori_loop(early, chunks, turn0, 0)
    first_move(chunks - 1).start()

    def own0(i, carry):
        part = at(i, chunk)
        mixed = transform(0, xv[part, 0:width], xv[part, width:both])
        move0[part] = mixed[:, :width]
        stay0[part] = mixed[:, width:]
        return carry

    lax.fori_loop(0, early, own0, 0)

    cos_moves[0].wait_recv()
    mix(1, cosin[0])
    raw_move.wait_recv()
    clear()

    def early0(i, carry):
        part = at(i, chunk)
        mixed = transform(1, raw[part, 0:width], raw[part, width:both])
        come0[part] = mixed[:, :width]
        rest[part] = mixed[:, width:]
        add_gram(mixed[:, :width], stay0[part])
        return carry

    lax.fori_loop(0, early, early0, 0)

    def gram1(i, carry):
        first_move(i).wait_recv()
        part = at(i, chunk)
        add_gram(come0[part], stay0[part])
        return carry

    lax.fori_loop(early, chunks, gram1, 0)
    skip_move.start()

    @pl.when(odd)
    def _():
        hold_move.start()

    @pl.when(jnp.logical_not(odd))
    def _():
        give_move.start()

    exchange(1)

    def turn1(i, carry):
        part = at(i, chunk)
        mixed = transform(0, come0[part], stay0[part])
        out_ref[part, 0:width] = mixed[:, :width]
        move1[part] = mixed[:, width:]

        @pl.when(i > given)
        def _():
            second_move(i - 1).start()

        return carry

    lax.fori_loop(given, chunks, turn1, 0)
    second_move(chunks - 1).start()

    @pl.when(jnp.logical_not(odd))
    def _():
        hold_move.wait_recv()
        pass_move.start()


    def own1(i, carry):
        part = at(i, chunk)
        out_ref[part, 0:width] = transform(0, come0[part], stay0[part])[:, :width]
        return carry

    lax.fori_loop(0, given, own1, 0)
    cos_moves[1].wait_recv()
    mix(1, cosin[1])
    skip_move.wait_recv()
    give_move.wait_recv()

    def early1(i, carry):
        part = at(i, chunk)
        out_ref[part, width:both] = transform(1, skip[part], rest[part])[:, width:]
        return carry

    lax.fori_loop(0, given, early1, 0)

    mgath[blk] = measure[...]

    def tell(k, carry):
        message(blk, lax.rem(blk + k, blk_count)).start()
        return carry

    lax.fori_loop(1, blk_count, tell, 0)

    def hear(k, carry):
        peer = lax.rem(blk + k, blk_count)
        message(peer, peer).wait_recv()
        return carry

    lax.fori_loop(1, blk_count, hear, 0)
    means = jnp.sum(mgath[...], axis=0) / float(blk_count)
    for step in range(STEPS):
        off_ref[step] = jnp.max(means[step:step + 1])

    def finish(i, carry):
        second_move(i).wait_send()
        second_move(i).wait_recv()
        return carry

    def sent(i, carry):
        first_move(i).wait_send()
        return carry

    lax.fori_loop(early, chunks, sent, 0)
    lax.fori_loop(given, chunks, finish, 0)

    @pl.when(odd)
    def _():
        hold_move.wait_send()

    @pl.when(jnp.logical_not(odd))
    def _():
        give_move.wait_send()
        pass_move.wait_send()

    raw_move.wait_send()
    skip_move.wait_send()
    for cos_move in cos_moves:
        cos_move.wait_send()

    def told(k, carry):
        message(blk, lax.rem(blk + k, blk_count)).wait_send()
        return carry

    lax.fori_loop(1, blk_count, told, 0)


def on_device(row_count, blk_count, matrix):
    rows, both = matrix.shape
    width = both // 2
    chunks, early, given = 16, 2, 4
    chunk = rows // chunks
    gram_chunk = rows // 8
    dma = pltpu.SemaphoreType.DMA
    block = pltpu.VMEM((rows, width), F32)
    some = pltpu.VMEM((given * chunk, width), F32)
    return pl.pallas_call(
        functools.partial(kernel, row_count, blk_count, chunk, gram_chunk, early, given),
        out_shape=(
            jax.ShapeDtypeStruct((rows, both), F32),
            jax.ShapeDtypeStruct((STEPS,), F32),
        ),
        in_specs=[pl.BlockSpec(memory_space=pltpu.HBM)],
        out_specs=(
            pl.BlockSpec(memory_space=pltpu.VMEM),
            pl.BlockSpec(memory_space=pltpu.SMEM),
        ),
        scratch_shapes=[
            pltpu.VMEM((rows, both), F32),
            block, block, block, block,
            pltpu.VMEM((early * chunk, both), F32),
            some, some,
            pltpu.VMEM(((given - early) * chunk, width), F32),
            pltpu.VMEM((both, both), F32),
            pltpu.VMEM((16, width), F32),
            pltpu.VMEM((STEPS, row_count, width + 16, width), F32),
            pltpu.VMEM((2, 2, both, both), BF16),
            pltpu.VMEM((STEPS, width, width), F32),
            pltpu.VMEM((STEPS, width, width), F32),
            pltpu.VMEM((8, width), F32),
            pltpu.VMEM((blk_count, 8, width), F32),
            dma((rows // gram_chunk,)),
            dma((chunks,)), dma((chunks,)), dma((chunks,)), dma((chunks,)),
            dma((STEPS, row_count)), dma((STEPS, row_count)),
            dma((blk_count,)), dma((blk_count,)),
            dma((5 + STEPS,)), dma((5 + STEPS,)),
        ],
        compiler_params=pltpu.CompilerParams(
            collective_id=0, has_side_effects=True, vmem_limit_bytes=48 * 1024 * 1024
        ),
    )(matrix)


def solution(mesh):
    return jax.shard_map(
        functools.partial(on_device, mesh.shape["row"], mesh.shape["blk"]),
        mesh=mesh,
        in_specs=(P("row", "blk"),),
        out_specs=(P("row", "blk"), P()),
        check_vma=False,
    )
```

```python
import functools

import jax
import jax.numpy as jnp
from jax import lax
from jax.experimental import pallas as pl
from jax.experimental.pallas import tpu as pltpu
from jax.sharding import PartitionSpec as P

STEPS = 2
NS_ITERS = 4
MESH = pl.DeviceIdType.MESH
F32 = jnp.float32
BF16 = jnp.bfloat16


def split(value):
    high = value.astype(BF16)
    return high, (value - high.astype(F32)).astype(BF16)


def dot(a, b):
    return jnp.dot(a, b, preferred_element_type=F32)


def product(a, b):
    ah, al = split(a)
    bh, bl = split(b)
    width = b.shape[1]
    both = dot(
        jnp.concatenate([ah, al], axis=1),
        jnp.concatenate(
            [
                jnp.concatenate([bh, bl], axis=1),
                jnp.concatenate([bh, jnp.zeros_like(bl)], axis=1),
            ],
            axis=0,
        ),
    )
    return both[:, :width] + both[:, width:]


def mixing(cosines):
    width = cosines.shape[0]
    rows = lax.broadcasted_iota(jnp.int32, (width, width), 0)
    columns = lax.broadcasted_iota(jnp.int32, (width, width), 1)
    identity = jnp.where(rows == columns, 1.0, 0.0).astype(F32)
    coupling = 0.5 * cosines
    flipped = coupling.T
    scale = 1.0 + jnp.sum(coupling * coupling, keepdims=True)
    shrink = 1.0 / scale
    current = [
        (identity + product(coupling, flipped)) * shrink,
        (identity + product(flipped, coupling)) * shrink,
    ]
    result = [None, None]
    for count in range(NS_ITERS):
        for side in range(2):
            y, z = current[side], result[side]
            inner = y if z is None else product(z, y)
            factor = 1.5 * identity - 0.5 * inner
            if count < NS_ITERS - 1:
                current[side] = product(y, factor)
            result[side] = factor if z is None else product(factor, z)
    root = 1.0 / jnp.sqrt(scale)
    first, second = result[0] * root, result[1] * root
    return (
        jnp.concatenate([first, product(coupling, second)], axis=1),
        jnp.concatenate([-product(flipped, first), second], axis=1),
    )


def kernel(
    row_count, blk_count, chunk, gram_chunk, early, given, direct,
    x_hbm, out_ref, off_ref,
    xv, move0, stay0, come0, move1, raw, rest, skip, hold, lent,
    acc, norms, gath, weights, coses, cosin, measure, mgath,
    load_sem, send0, recv0, send1, recv1, gsend, grecv, msend, mrecv, esend, erecv,
):
    rows, both = x_hbm.shape
    width = both // 2
    chunks = rows // chunk
    row, blk = lax.axis_index("row"), lax.axis_index("blk")
    after = lax.rem(blk + 1, blk_count)
    second = lax.rem(blk + 2, blk_count)
    odd = lax.rem(blk, 2) == 1
    below = lax.rem(blk + blk_count - 1, blk_count)
    early_rows = pl.ds(0, early * chunk)
    given_rows = pl.ds(early * chunk, (given - early) * chunk)

    barrier = pltpu.get_barrier_semaphore()
    for k in range(1, row_count):
        pl.semaphore_signal(
            barrier, inc=1, device_id={"row": lax.rem(row + k, row_count)}, device_id_type=MESH
        )

    def greet(k, carry):
        pl.semaphore_signal(
            barrier, inc=1, device_id={"blk": lax.rem(blk + k, blk_count)}, device_id_type=MESH
        )
        return carry

    lax.fori_loop(1, blk_count, greet, 0)

    def at(i, size):
        return pl.ds(pl.multiple_of(i * size, size), size)

    def load(i):
        return pltpu.make_async_copy(
            x_hbm.at[at(i, gram_chunk)], xv.at[at(i, gram_chunk)], load_sem.at[i]
        )

    def start_load(i, carry):
        load(i).start()
        return carry

    lax.fori_loop(0, rows // gram_chunk, start_load, 0)

    def ahead(source, target, k, peer, sender=None):
        sender = k if sender is None else sender
        return pltpu.make_async_remote_copy(
            src_ref=source, dst_ref=target, send_sem=esend.at[sender], recv_sem=erecv.at[k],
            device_id={"blk": peer}, device_id_type=MESH,
        )

    raw_move = ahead(x_hbm.at[early_rows], raw, 0, after)
    skip_move = ahead(move0.at[pl.ds(0, given * chunk)], skip, 1, second)
    give_move = ahead(stay0.at[given_rows], rest.at[given_rows], 2 + STEPS, after)
    hold_move = ahead(stay0.at[given_rows], hold, 3 + STEPS, below)
    late_rows = pl.ds(given * chunk, (direct - given) * chunk)
    lend_move = ahead(move1.at[late_rows], lent, 5 + STEPS, below)
    land_move = ahead(lent, out_ref.at[late_rows, pl.ds(width, width)], 6 + STEPS, second)
    pass_move = ahead(hold, rest.at[given_rows], 2 + STEPS, second, 4 + STEPS)
    cos_moves = [ahead(coses.at[s], cosin.at[s], 2 + s, after) for s in range(STEPS)]

    pl.semaphore_wait(barrier, row_count + blk_count - 2)
    raw_move.start()

    def add_gram(left, right):
        lh, ll = split(left)
        rh, rl = split(right)
        acc[...] += lax.dot_general(
            jnp.concatenate([lh, ll], axis=1),
            jnp.concatenate([rh, rl], axis=1),
            (((0,), (0,)), ((), ())),
            preferred_element_type=F32,
        )
        norms[0:8] += jnp.sum((left * left).reshape(-1, 8, width), axis=0)
        norms[8:16] += jnp.sum((right * right).reshape(-1, 8, width), axis=0)

    def clear():
        acc[...] = jnp.zeros_like(acc)
        norms[...] = jnp.zeros_like(norms)

    def mix(slot, cosines):
        top, bottom = mixing(cosines)
        high, low = split(top)
        weights[slot, 0, :width] = high
        weights[slot, 1, :width] = low
        high, low = split(bottom)
        weights[slot, 0, width:] = high
        weights[slot, 1, width:] = low

    def exchange(step):
        def copy(owner, peer, k):
            return pltpu.make_async_remote_copy(
                src_ref=gath.at[step, owner],
                dst_ref=gath.at[step, owner],
                send_sem=gsend.at[step, k],
                recv_sem=grecv.at[step, owner],
                device_id={"row": peer},
                device_id_type=MESH,
            )

        gath[step, row, 0:width] = (
            acc[:width, :width] + acc[:width, width:] + acc[width:, :width]
        ) + acc[width:, width:]
        first = jnp.sum(norms[0:8], axis=0, keepdims=True)
        second = jnp.sum(norms[8:16], axis=0, keepdims=True)
        gath[step, row, width:width + 8] = jnp.broadcast_to(first, (8, width))
        gath[step, row, width + 8:width + 16] = jnp.broadcast_to(second, (8, width))
        for k in range(1, row_count):
            copy(row, lax.rem(row + k, row_count), k).start()
        for k in range(1, row_count):
            peer = lax.rem(row + k, row_count)
            copy(peer, peer, k).wait_recv()
        total = gath[step, 0]
        for r in range(1, row_count):
            total = total + gath[step, r]
        for k in range(1, row_count):
            copy(row, lax.rem(row + k, row_count), k).wait_send()
        cross = total[:width]
        first = lax.rsqrt(jnp.broadcast_to(total[width:width + 1], (width, width))).T
        second = lax.rsqrt(jnp.broadcast_to(total[width + 8:width + 9], (width, width)))
        cosines = cross * first * second
        measure[step:step + 1] = jnp.broadcast_to(
            jnp.sum(cosines * cosines, keepdims=True), (1, width)
        )
        coses[step] = cosines
        cos_moves[step].start()
        mix(0, cosines)

    def transform(slot, left, right):
        lh, ll = split(left)
        rh, rl = split(right)
        high = jnp.concatenate([lh, rh], axis=1)
        low = jnp.concatenate([ll, rl], axis=1)
        own, fine = weights[slot, 0], weights[slot, 1]
        return dot(high, own) + (dot(high, fine) + dot(low, own))

    def first_move(i):
        return pltpu.make_async_remote_copy(
            src_ref=move0.at[at(i, chunk)], dst_ref=come0.at[at(i, chunk)],
            send_sem=send0.at[i], recv_sem=recv0.at[i],
            device_id={"blk": after}, device_id_type=MESH,
        )

    def second_move(i):
        return pltpu.make_async_remote_copy(
            src_ref=move1.at[at(i, chunk)], dst_ref=out_ref.at[at(i, chunk), pl.ds(width, width)],
            send_sem=send1.at[i], recv_sem=recv1.at[i],
            device_id={"blk": after}, device_id_type=MESH,
        )

    def message(owner, peer):
        return pltpu.make_async_remote_copy(
            src_ref=mgath.at[owner], dst_ref=mgath.at[owner],
            send_sem=msend.at[peer], recv_sem=mrecv.at[owner],
            device_id={"blk": peer}, device_id_type=MESH,
        )

    clear()

    def gram0(i, carry):
        load(i).wait()
        part = at(i, gram_chunk)
        add_gram(xv[part, 0:width], xv[part, width:both])
        return carry

    lax.fori_loop(0, rows // gram_chunk, gram0, 0)
    measure[...] = jnp.zeros_like(measure)
    exchange(0)

    def turn0(i, carry):
        part = at(i, chunk)
        mixed = transform(0, xv[part, 0:width], xv[part, width:both])
        move0[part] = mixed[:, :width]
        stay0[part] = mixed[:, width:]

        @pl.when(i > early)
        def _():
            first_move(i - 1).start()

        return carry

    lax.fori_loop(early, chunks, turn0, 0)
    first_move(chunks - 1).start()

    def own0(i, carry):
        part = at(i, chunk)
        mixed = transform(0, xv[part, 0:width], xv[part, width:both])
        move0[part] = mixed[:, :width]
        stay0[part] = mixed[:, width:]
        return carry

    lax.fori_loop(0, early, own0, 0)

    cos_moves[0].wait_recv()
    mix(1, cosin[0])
    raw_move.wait_recv()
    clear()

    def early0(i, carry):
        part = at(i, chunk)
        mixed = transform(1, raw[part, 0:width], raw[part, width:both])
        come0[part] = mixed[:, :width]
        rest[part] = mixed[:, width:]
        add_gram(mixed[:, :width], stay0[part])
        return carry

    lax.fori_loop(0, early, early0, 0)

    def gram1(i, carry):
        first_move(i).wait_recv()
        part = at(i, chunk)
        add_gram(come0[part], stay0[part])
        return carry

    lax.fori_loop(early, chunks, gram1, 0)
    skip_move.start()

    @pl.when(odd)
    def _():
        hold_move.start()

    @pl.when(jnp.logical_not(odd))
    def _():
        give_move.start()

    exchange(1)

    def turn1(i, carry):
        part = at(i, chunk)
        mixed = transform(0, come0[part], stay0[part])
        out_ref[part, 0:width] = mixed[:, :width]
        move1[part] = mixed[:, width:]

        @pl.when(jnp.logical_or(i > direct, jnp.logical_and(i > given, jnp.logical_not(odd))))
        def _():
            second_move(i - 1).start()

        @pl.when(jnp.logical_and(i == direct, odd))
        def _():
            lend_move.start()

        return carry

    lax.fori_loop(given, chunks, turn1, 0)
    second_move(chunks - 1).start()

    @pl.when(jnp.logical_not(odd))
    def _():
        hold_move.wait_recv()
        pass_move.start()
        lend_move.wait_recv()
        land_move.start()


    def own1(i, carry):
        part = at(i, chunk)
        out_ref[part, 0:width] = transform(0, come0[part], stay0[part])[:, :width]
        return carry

    lax.fori_loop(0, given, own1, 0)
    cos_moves[1].wait_recv()
    mix(1, cosin[1])
    skip_move.wait_recv()
    give_move.wait_recv()

    def early1(i, carry):
        part = at(i, chunk)
        out_ref[part, width:both] = transform(1, skip[part], rest[part])[:, width:]
        return carry

    lax.fori_loop(0, given, early1, 0)

    mgath[blk] = measure[...]

    def tell(k, carry):
        message(blk, lax.rem(blk + k, blk_count)).start()
        return carry

    lax.fori_loop(1, blk_count, tell, 0)

    def hear(k, carry):
        peer = lax.rem(blk + k, blk_count)
        message(peer, peer).wait_recv()
        return carry

    lax.fori_loop(1, blk_count, hear, 0)
    means = jnp.sum(mgath[...], axis=0) / float(blk_count)
    for step in range(STEPS):
        off_ref[step] = jnp.max(means[step:step + 1])

    def finish(i, carry):
        second_move(i).wait_send()
        second_move(i).wait_recv()
        return carry

    def sent(i, carry):
        first_move(i).wait_send()
        return carry

    lax.fori_loop(early, chunks, sent, 0)
    lax.fori_loop(direct, chunks, finish, 0)

    @pl.when(odd)
    def _():
        def arrived(i, carry):
            second_move(i).wait_recv()
            return carry

        lax.fori_loop(given, direct, arrived, 0)
        lend_move.wait_send()

    @pl.when(jnp.logical_not(odd))
    def _():
        def left(i, carry):
            second_move(i).wait_send()
            return carry

        lax.fori_loop(given, direct, left, 0)
        land_move.wait_send()
        land_move.wait_recv()

    @pl.when(odd)
    def _():
        hold_move.wait_send()

    @pl.when(jnp.logical_not(odd))
    def _():
        give_move.wait_send()
        pass_move.wait_send()

    raw_move.wait_send()
    skip_move.wait_send()
    for cos_move in cos_moves:
        cos_move.wait_send()

    def told(k, carry):
        message(blk, lax.rem(blk + k, blk_count)).wait_send()
        return carry

    lax.fori_loop(1, blk_count, told, 0)


def on_device(row_count, blk_count, matrix):
    rows, both = matrix.shape
    width = both // 2
    chunks, early, given, direct = 16, 3, 5, 7
    chunk = rows // chunks
    gram_chunk = rows // 8
    dma = pltpu.SemaphoreType.DMA
    block = pltpu.VMEM((rows, width), F32)
    some = pltpu.VMEM((given * chunk, width), F32)
    return pl.pallas_call(
        functools.partial(kernel, row_count, blk_count, chunk, gram_chunk, early, given, direct),
        out_shape=(
            jax.ShapeDtypeStruct((rows, both), F32),
            jax.ShapeDtypeStruct((STEPS,), F32),
        ),
        in_specs=[pl.BlockSpec(memory_space=pltpu.HBM)],
        out_specs=(
            pl.BlockSpec(memory_space=pltpu.VMEM),
            pl.BlockSpec(memory_space=pltpu.SMEM),
        ),
        scratch_shapes=[
            pltpu.VMEM((rows, both), F32),
            block, block, block, block,
            pltpu.VMEM((early * chunk, both), F32),
            some, some,
            pltpu.VMEM(((given - early) * chunk, width), F32),
            pltpu.VMEM(((direct - given) * chunk, width), F32),
            pltpu.VMEM((both, both), F32),
            pltpu.VMEM((16, width), F32),
            pltpu.VMEM((STEPS, row_count, width + 16, width), F32),
            pltpu.VMEM((2, 2, both, both), BF16),
            pltpu.VMEM((STEPS, width, width), F32),
            pltpu.VMEM((STEPS, width, width), F32),
            pltpu.VMEM((8, width), F32),
            pltpu.VMEM((blk_count, 8, width), F32),
            dma((rows // gram_chunk,)),
            dma((chunks,)), dma((chunks,)), dma((chunks,)), dma((chunks,)),
            dma((STEPS, row_count)), dma((STEPS, row_count)),
            dma((blk_count,)), dma((blk_count,)),
            dma((7 + STEPS,)), dma((7 + STEPS,)),
        ],
        compiler_params=pltpu.CompilerParams(
            collective_id=0, has_side_effects=True, vmem_limit_bytes=48 * 1024 * 1024
        ),
    )(matrix)


def solution(mesh):
    return jax.shard_map(
        functools.partial(on_device, mesh.shape["row"], mesh.shape["blk"]),
        mesh=mesh,
        in_specs=(P("row", "blk"),),
        out_specs=(P("row", "blk"), P()),
        check_vma=False,
    )
```
